256 devices in a mesh: ang: 32 (over y_lo, z, core), ax: 8 (over x, y_hi).
Axes of the slice: x: 4, y: 4 (y_hi: 2, y_lo: 2; y = y_hi * 2 + y_lo), z: 8, core: 2. Of those that a mesh axis runs over, the one named last changes fastest.
Arguments:
- concentration: float32 [3, 1024, 128, 512], P(None, 'ang', 'ax'), may hold values from 0.1 to 2
- courant: float32 [512], replicated, may hold values from 0.1 to 0.35
- axial_diffusion: float32 [3], replicated, may hold values from 0.05 to 0.12
- angular_rate: float32 [3, 512], replicated, may hold values from 0.05 to 0.18
- rate_constants: float32 [4], replicated, may hold values from 0.05 to 0.2
- species_map: int32 [4, 3], replicated, may hold values from 0 to 2, each once within a row
- wall_flags: int32 [3, 1024], P(None, 'ang'), may hold values 0 or 1
- radial_inverse: bfloat16 [3, 1024, 1024], replicated, may hold values from -1 to 1, as said below
Outputs:
- final_field: float32 [3, 1024, 128, 512], P(None, 'ang', 'ax')
The draws below stay inside these ranges and needn't reach their ends.
Inputs may be any that keep to these rules, and one draw needn't show every extreme that they name: Every matrix is centrosymmetric: radial_inverse[s, i, j] equals radial_inverse[s, 1023 - i, 1023 - j].
All inputs are finite; a program needn't handle non-finite values. No bound on the sum of `wall_flags` on one device may be relied on, other than what follows from the above.
Results may differ from the reference program's by a relative error of at most 0.0029.
Values may be sent and summed in bfloat16 or wider, within the bound.
A program may use at most 64 MiB of HBM per device.

```python
import math
import jax
import jax.numpy as jnp
from jax import lax

NSPEC = 3
NREACT = 4
NRAD = 1024
HALF = 512
STEPS = 2
ANG = 1024
PLANES = 128


def draw_radial_inverse(key, part):
    spread = 0.6 / math.sqrt(NRAD)
    base = jax.random.normal(key, (NSPEC, NRAD, NRAD), jnp.float32)
    coupling = jnp.clip(base * spread, -0.1, 0.1)
    coupling = 0.5 * (coupling + coupling[:, ::-1, ::-1])
    matrix = coupling + 0.8 * jnp.eye(NRAD, dtype=jnp.float32)[None]
    return matrix.astype(jnp.bfloat16)


def plant(array, stream_key, low, high):
    spot = [jax.random.randint(jax.random.fold_in(stream_key, axis), (), 0, length) for axis, length in enumerate(array.shape)]
    widest = array.shape.index(max(array.shape))
    neighbour = spot[:widest] + [(spot[widest] + 1) % array.shape[widest]] + spot[widest + 1:]
    return array.at[tuple(spot)].set(low).at[tuple(neighbour)].set(high)


def steps_of(stream_key, shape, split, least, largest):
    gain = 1.0
    for position, blocks in split:
        draws = jax.random.uniform(jax.random.fold_in(jax.random.fold_in(stream_key, 6), position), (blocks,), jnp.float32, least / len(split), largest / len(split))
        gain = gain * jnp.repeat(jnp.exp(draws), shape[position] // blocks).reshape((-1,) + (1,) * (len(shape) - 1 - position))
    return gain


def setup_inputs(seed: int = 0) -> dict:
    key_of = jax.random.split(jax.random.key(seed), 9)
    concentration = jnp.clip(0.1 + 1.9 * jax.random.uniform(key_of[0], (NSPEC, ANG, PLANES, HALF), jnp.float32) ** steps_of(key_of[0], (NSPEC, ANG, PLANES, HALF), ((1, 32), (2, 8)), -0.2, 0.2), 0.1, 2.0)
    courant = jnp.clip(jax.random.uniform(key_of[1], (HALF,), jnp.float32, 0.1, 0.35), 0.1, 0.35)
    axial_diffusion = jnp.clip(jax.random.uniform(key_of[2], (NSPEC,), jnp.float32, 0.05, 0.12), 0.05, 0.12)
    angular_rate = jnp.clip(jnp.exp(jax.random.uniform(key_of[3], (NSPEC, HALF), jnp.float32, math.log(0.05), math.log(0.18))), 0.05, 0.18)
    rate_constants = jnp.clip(jnp.exp(jax.random.uniform(key_of[4], (NREACT,), jnp.float32, math.log(0.05), math.log(0.2))), 0.05, 0.2)
    species_map = jax.vmap(lambda own: jax.random.permutation(own, NSPEC))(jax.random.split(key_of[5], NREACT)).reshape((NREACT, NSPEC)).astype(jnp.int32)
    wall_flags = plant((jax.random.randint(key_of[6], (NSPEC, ANG), 0, 2) < 1).astype(jnp.int32), jax.random.fold_in(key_of[6], 1), 0, 1)
    radial_inverse = draw_radial_inverse(jax.random.fold_in(key_of[8], 71), 0)
    return {"concentration": concentration, "courant": courant, "axial_diffusion": axial_diffusion, "angular_rate": angular_rate, "rate_constants": rate_constants, "species_map": species_map, "wall_flags": wall_flags, "radial_inverse": radial_inverse}


def species_step(field, species, courant, axial_diffusion, angular_rate, rate_constants, species_map, wall_flags, radial_inverse):
    own_part = field[species]
    angle_before = jnp.roll(own_part, 1, 0)
    angle_after = jnp.roll(own_part, -1, 0)
    zero_plane = jnp.zeros_like(own_part[:, :1])
    axial_before = jnp.concatenate([zero_plane, own_part[:, :-1]], 1)
    axial_after = jnp.concatenate([own_part[:, 1:], zero_plane], 1)
    reaction = jnp.zeros_like(own_part)
    for which_reaction in range(NREACT):
        first_index = species_map[which_reaction, 0]
        second_index = species_map[which_reaction, 1]
        product_index = species_map[which_reaction, 2]
        rate_term = rate_constants[which_reaction] * field[first_index] * field[second_index]
        weight = (product_index == species).astype(own_part.dtype) - (first_index == species).astype(own_part.dtype) - (second_index == species).astype(own_part.dtype)
        reaction = reaction + weight * rate_term
    explicit = (own_part - courant * (own_part - axial_before)
                + axial_diffusion[species] * (axial_after - 2.0 * own_part + axial_before)
                + angular_rate[species] * (angle_after - 2.0 * own_part + angle_before)
                + reaction)
    opposite = jnp.roll(explicit, -(ANG // 2), 0)[:, :, ::-1]
    diameter = jnp.concatenate([explicit, opposite], 2).astype(jnp.bfloat16)
    rows_block = radial_inverse[species, :HALF, :]
    implicit = jnp.dot(diameter.reshape(-1, NRAD), jnp.transpose(rows_block), preferred_element_type=jnp.float32).reshape(explicit.shape)
    wall_mask = lax.broadcasted_iota(jnp.int32, implicit.shape, 2) == 0
    wall_value = jnp.where(wall_flags[species][:, None, None] == 1, 0.0, implicit[:, :, 1:2])
    return jnp.where(wall_mask, wall_value, implicit)


def reference(concentration, courant, axial_diffusion, angular_rate, rate_constants, species_map, wall_flags, radial_inverse):
    field = concentration
    for step_index in range(STEPS):
        current = field
        field = lax.map(lambda species: species_step(current, species, courant, axial_diffusion, angular_rate, rate_constants, species_map, wall_flags, radial_inverse), jnp.arange(NSPEC, dtype=jnp.int32))
    return field
```

```python
import functools

import jax
import jax.numpy as jnp
from jax import lax
from jax.experimental import pallas as pl
from jax.experimental.pallas import tpu as pltpu
from jax.sharding import PartitionSpec as P

MESH = pl.DeviceIdType.MESH
F32, BF16 = jnp.float32, jnp.bfloat16
LANES = 128
H = 2


def comm_kernel(
    conc, courant, ang_rate, ax_diff, rates, smap, flags, rinv,
    diam_out, w_out,
    o0, o1, t0, t1, ob, d1, d2, w, ma, ml, coef, hxf, pkf, pkb, hx, pa, ha, fl, fl_other, keep,
    load_sem, x_send, x_recv, hx_send, hx_recv, a_send, a_recv, fl_sem, m_sem, w_sem, d_sem,
):
    species, _, planes, radial = o0.shape
    angles = ob.shape[1]
    chunks = angles // (2 * H)
    rows_q = 2 * H
    per_blk = species * rows_q
    ang, ax = lax.axis_index("ang"), lax.axis_index("ax")
    n_ang, n_ax = lax.axis_size("ang"), lax.axis_size("ax")
    opp = lax.rem(ang + n_ang // 2, n_ang)
    up, down = lax.rem(ang + 1, n_ang), lax.rem(ang + n_ang - 1, n_ang)
    has_low, has_high = ax > 0, ax < n_ax - 1
    peer = {"ang": opp, "ax": ax}
    ang_peers = ({"ang": up, "ax": ax}, {"ang": down, "ax": ax})
    ax_peers = ({"ang": opp, "ax": ax + 1}, {"ang": opp, "ax": ax - 1})
    has_to, has_from = (has_high, has_low), (has_low, has_high)
    own, other = (o0, o1), (t0, t1)

    def low(j):
        return j * H

    def high(j):
        return angles - (j + 1) * H

    def angle(j, q):
        return j * H + q if q < H else angles - (j + 1) * H + q - H

    def load(j, end):
        start = (low, high)[end](j)
        return pltpu.make_async_copy(
            conc.at[:, pl.ds(start, H)], o0.at[:, pl.ds(start + 1, H)], load_sem.at[j, end]
        )

    def exchange(j, end):
        start = (low, high)[end](j)
        return pltpu.make_async_remote_copy(
            ob.at[:, pl.ds(start, H)], t0.at[:, pl.ds(start + 1, H)],
            x_send.at[j, end], x_recv.at[j, end], device_id=peer, device_id_type=MESH,
        )

    def ax_copy(step, j, side):
        return pltpu.make_async_remote_copy(
            pkb.at[step, j, side], hx.at[step, j, side],
            hx_send.at[step, j, side], hx_recv.at[step, j, side],
            device_id=ax_peers[side], device_id_type=MESH,
        )

    def ang_copies(step, side):
        t = other[step]
        source, target = ((angles, 0), (1, angles + 1))[side]
        return (
            pltpu.make_async_remote_copy(
                pa.at[step, side], ha.at[step, side],
                a_send.at[step, side, 0], a_recv.at[step, side, 0],
                device_id=ang_peers[side], device_id_type=MESH,
            ),
            pltpu.make_async_remote_copy(
                t.at[:, source], t.at[:, target],
                a_send.at[step, side, 1], a_recv.at[step, side, 1],
                device_id=ang_peers[side], device_id_type=MESH,
            ),
        )

    def flag_copy():
        return pltpu.make_async_remote_copy(
            fl, fl_other, fl_sem.at[0], fl_sem.at[1], device_id=peer, device_id_type=MESH
        )

    def diam_copy(j, end):
        start = (low, high)[end](j)
        return pltpu.make_async_copy(
            d2.at[:, pl.ds(start, H)], diam_out.at[:, pl.ds(start, H)], d_sem.at[j, end]
        )

    @pl.loop(0, chunks)
    def _(j):
        load(j, 0).start()
        load(j, 1).start()

    load_a = pltpu.make_async_copy(rinv.at[:, :radial, :radial], ma, m_sem.at[0])
    load_l = pltpu.make_async_copy(rinv.at[:, radial:, :radial], ml, m_sem.at[1])
    load_a.start()
    load_l.start()

    barrier = pltpu.get_barrier_semaphore()
    for device in (peer, *ang_peers):
        pl.semaphore_signal(barrier, inc=1, device_id=device, device_id_type=MESH)
    for side in range(2):

        @pl.when(has_to[side])
        def _():
            pl.semaphore_signal(barrier, inc=1, device_id=ax_peers[side], device_id_type=MESH)

    fl[...] = jnp.zeros_like(fl)
    fl[:species, :angles] = flags[...].astype(F32)
    for s in range(species):
        diffusion = ax_diff[s]
        coef[s, 0] = jnp.broadcast_to(
            1.0 - courant[...] - 2.0 * diffusion - 2.0 * ang_rate[s : s + 1], (planes, radial)
        )
        coef[s, 1] = jnp.broadcast_to(courant[...] + diffusion, (planes, radial))
        coef[s, 2] = jnp.broadcast_to(ang_rate[s : s + 1], (planes, radial))
    for side in range(2):

        @pl.when(jnp.logical_not(has_from[side]))
        def _():
            for step in range(2):

                @pl.loop(0, chunks)
                def _(j):
                    hx[step, j, side] = jnp.zeros(hx.shape[3:], BF16)

    gains = []
    for p in range(species):
        gain = jnp.float32(0.0)
        for k in range(rates.shape[0]):
            gain = gain + jnp.where(smap[k, 2] == p, rates[k], jnp.float32(0.0))
        gains.append(gain)

    def cast(j):
        for end in range(2):
            load(j, end).wait()
            start = (low, high)[end](j)
            for i in range(H):
                for s in range(species):
                    ob[s, start + i] = o0[s, start + i + 1].astype(BF16)

    cast(0)
    pl.semaphore_wait(barrier, 3 + jnp.where(has_low, 1, 0) + jnp.where(has_high, 1, 0))
    exchange(0, 0).start()
    exchange(0, 1).start()
    flag_copy().start()

    @pl.loop(1, chunks)
    def _(j):
        cast(j)
        exchange(j, 0).start()
        exchange(j, 1).start()

    load_a.wait()
    load_l.wait()
    flip = (
        lax.broadcasted_iota(jnp.int32, (radial, radial), 0)
        + lax.broadcasted_iota(jnp.int32, (radial, radial), 1)
        == radial - 1
    )
    flip = jnp.where(flip, 1.0, 0.0).astype(BF16)
    for s in range(species):
        w[s, :radial] = ma[s].T
        w[s, radial:] = jnp.dot(ml[s].T, flip, preferred_element_type=F32).astype(BF16)
    w_copy = pltpu.make_async_copy(w, w_out, w_sem.at[0])
    w_copy.start()

    flag_copy().wait_recv()
    diagonal = lax.broadcasted_iota(jnp.int32, (angles, LANES), 0) == lax.broadcasted_iota(
        jnp.int32, (angles, LANES), 1
    )
    for blk, ref in enumerate((fl, fl_other)):
        for s in range(species):
            row = jnp.broadcast_to(ref[s : s + 1], (angles, LANES))
            column = jnp.sum(jnp.where(diagonal, row, 0.0), axis=1, keepdims=True)
            rows = jnp.broadcast_to(1.0 - column, (angles, LANES))
            for a in range(angles):
                keep[blk, s, a] = jnp.broadcast_to(rows[a : a + 1], (planes, LANES))

    lane0 = lax.broadcasted_iota(jnp.int32, (planes, LANES), 1) == 0
    plane = lax.broadcasted_iota(jnp.int32, (planes, LANES), 0)
    first, last = plane == 0, plane == planes - 1

    def forward(step, j):
        for q in range(rows_q):
            a = angle(j, q) + 1
            for blk, ref in ((1, own[step]), (0, other[step])):
                for s in range(species):
                    value = ref[s, a].astype(F32)
                    row = slice(blk * per_blk + s * rows_q + q, blk * per_blk + s * rows_q + q + 1)
                    pkf[0, row, :] = value[planes - 1 : planes]
                    pkf[1, row, :] = value[0:1]

        for side in range(2):
            pkb[step, j, side] = pkf[side].astype(BF16)

            @pl.when(has_to[side])
            def _():
                ax_copy(step, j, side).start()

    def send_edges(step):
        for side in range(2):
            source = (angles, 1)[side]
            for s in range(species):
                pa[step, side, s] = own[step][s, source].astype(BF16)
            for copy in ang_copies(step, side):
                copy.start()

    def take_edges(step):
        for side in range(2):
            for copy in ang_copies(step, side):
                copy.wait_recv()
            target = (0, angles + 1)[side]
            for s in range(species):
                own[step][s, target] = ha[step, side, s].astype(F32)

    def explicit(step, j, store):
        for side in range(2):

            @pl.when(has_from[side])
            def _():
                ax_copy(step, j, side).wait_recv()

            hxf[side] = hx[step, j, side].astype(F32)

        for q in range(rows_q):
            a = angle(j, q) + 1
            for blk, ref in ((0, own[step]), (1, other[step])):
                for lane in range(0, radial, LANES):
                    sl = pl.ds(lane, LANES)
                    f = [ref[s, a, :, sl].astype(F32) for s in range(species)]
                    terms = [
                        gains[s] * (f[(s + 1) % species] * f[(s + 2) % species])
                        for s in range(species)
                    ]
                    total = terms[0] + terms[1] + terms[2]
                    for s in range(species):
                        row = slice(blk * per_blk + s * rows_q + q, blk * per_blk + s * rows_q + q + 1)
                        before = jnp.where(first, hxf[0, row, sl], pltpu.roll(f[s], 1, 0))
                        after = jnp.where(last, hxf[1, row, sl], pltpu.roll(f[s], planes - 1, 0))
                        angular = ref[s, a - 1, :, sl].astype(F32) + ref[s, a + 1, :, sl].astype(F32)
                        value = (
                            coef[s, 0, :, sl] * f[s]
                            + coef[s, 1, :, sl] * before
                            + ax_diff[s] * after
                            + coef[s, 2, :, sl] * angular
                            + (2.0 * terms[s] - total)
                        )
                        store(q, a, blk, s, lane, value.astype(BF16))

    def store_first(q, a, blk, s, lane, value):
        half = rows_q * planes
        sl = pl.ds(lane, LANES)
        offset = q * planes
        d1[s, pl.ds(blk * half + offset, planes), sl] = value
        if blk == 0:
            d1[s, pl.ds(2 * half + offset, planes), sl] = value

    def store_second(q, a, blk, s, lane, value):
        d2[s, a - 1, :, pl.ds(blk * radial + lane, LANES)] = value

    def implicit(j):
        half = rows_q * planes
        for s in range(species):
            y = jnp.dot(d1[s, : 2 * half], w[s, :radial], preferred_element_type=F32)
            y = y + jnp.dot(d1[s, half:], w[s, radial:], preferred_element_type=F32)
            for blk, ref in ((0, o1), (1, t1)):
                for q in range(rows_q):
                    a = angle(j, q)
                    part = y[blk * half + q * planes : blk * half + (q + 1) * planes]
                    head = part[:, :LANES]
                    wall = pltpu.roll(head, LANES - 1, 1) * keep[blk, s, a]
                    ref[s, a + 1, :, :LANES] = jnp.where(lane0, wall, head).astype(ref.dtype)
                    ref[s, a + 1, :, LANES:] = part[:, LANES:].astype(ref.dtype)

    @pl.loop(0, chunks + 2)
    def _(i):
        @pl.when(i < chunks)
        def _():
            exchange(i, 0).wait_recv()
            exchange(i, 1).wait_recv()
            forward(0, i)

            @pl.when(i == 0)
            def _():
                send_edges(0)

        @pl.when(jnp.logical_and(i >= 1, i <= chunks))
        def _():
            @pl.when(i == 1)
            def _():
                take_edges(0)

            explicit(0, i - 1, store_first)
            implicit(i - 1)
            forward(1, i - 1)

            @pl.when(i == 1)
            def _():
                send_edges(1)

        @pl.when(i >= 2)
        def _():
            @pl.when(i == 2)
            def _():
                take_edges(1)

            explicit(1, i - 2, store_second)
            diam_copy(i - 2, 0).start()
            diam_copy(i - 2, 1).start()

    w_copy.wait()
    flag_copy().wait_send()
    for step in range(2):
        for side in range(2):
            for copy in ang_copies(step, side):
                copy.wait_send()

    @pl.loop(0, chunks)
    def _(j):
        for end in range(2):
            exchange(j, end).wait_send()
            diam_copy(j, end).wait()
        for step in range(2):
            for side in range(2):

                @pl.when(has_to[side])
                def _():
                    ax_copy(step, j, side).wait_send()


def final_kernel(planes, flags, diam, w, out):
    radial = out.shape[2]
    s, block = pl.program_id(0), pl.program_id(1)
    y = jnp.dot(diam[0], w[0], preferred_element_type=F32)
    out[0] = y
    lane0 = lax.broadcasted_iota(jnp.int32, (planes, LANES), 1) == 0
    count = out.shape[1] // planes
    for i in range(count):
        head = y[i * planes : (i + 1) * planes, :LANES]
        wall = jnp.where(flags[s, block * count + i] == 1, 0.0, pltpu.roll(head, LANES - 1, 1))
        out[0, pl.ds(i * planes, planes), :LANES] = jnp.where(lane0, wall, head)


def per_device(
    concentration, courant, axial_diffusion, angular_rate, rate_constants, species_map, wall_flags, radial_inverse
):
    species, angles, planes, radial = concentration.shape
    chunks, rows_q = angles // (2 * H), 2 * H
    packed = 2 * species * rows_q
    vmem = pl.BlockSpec(memory_space=pltpu.VMEM)
    smem = pl.BlockSpec(memory_space=pltpu.SMEM)
    anywhere = pl.BlockSpec(memory_space=pl.ANY)
    dma = pltpu.SemaphoreType.DMA
    diam, w = pl.pallas_call(
        comm_kernel,
        out_shape=(
            jax.ShapeDtypeStruct((species, angles, planes, 2 * radial), BF16),
            jax.ShapeDtypeStruct((species, 2 * radial, radial), BF16),
        ),
        in_specs=[anywhere, vmem, vmem, smem, smem, smem, vmem, anywhere],
        out_specs=(anywhere, anywhere),
        scratch_shapes=[
            pltpu.VMEM((species, angles + 2, planes, radial), F32),
            pltpu.VMEM((species, angles + 2, planes, radial), F32),
            pltpu.VMEM((species, angles + 2, planes, radial), BF16),
            pltpu.VMEM((species, angles + 2, planes, radial), BF16),
            pltpu.VMEM((species, angles, planes, radial), BF16),
            pltpu.VMEM((species, 3 * rows_q * planes, radial), BF16),
            pltpu.VMEM((species, angles, planes, 2 * radial), BF16),
            pltpu.VMEM((species, 2 * radial, radial), BF16),
            pltpu.VMEM((species, radial, radial), BF16),
            pltpu.VMEM((species, radial, radial), BF16),
            pltpu.VMEM((species, 3, planes, radial), F32),
            pltpu.VMEM((2, packed, radial), F32),
            pltpu.VMEM((2, packed, radial), F32),
            pltpu.VMEM((2, chunks, 2, packed, radial), BF16),
            pltpu.VMEM((2, chunks, 2, packed, radial), BF16),
            pltpu.VMEM((2, 2, species, planes, radial), BF16),
            pltpu.VMEM((2, 2, species, planes, radial), BF16),
            pltpu.VMEM((8, LANES), F32),
            pltpu.VMEM((8, LANES), F32),
            pltpu.VMEM((2, species, angles, planes, LANES), F32),
            dma((chunks, 2)),
            dma((chunks, 2)),
            dma((chunks, 2)),
            dma((2, chunks, 2)),
            dma((2, chunks, 2)),
            dma((2, 2, 2)),
            dma((2, 2, 2)),
            dma((2,)),
            dma((2,)),
            dma((1,)),
            dma((chunks, 2)),
        ],
        compiler_params=pltpu.CompilerParams(
            collective_id=0, has_side_effects=True, vmem_limit_bytes=48 * 1024 * 1024
        ),
        name="steps",
    )(
        concentration, courant.reshape(1, radial), angular_rate, axial_diffusion, rate_constants,
        species_map, wall_flags, radial_inverse,
    )
    rows = angles * planes
    block = min(rows, 256)
    out = pl.pallas_call(
        functools.partial(final_kernel, planes),
        out_shape=jax.ShapeDtypeStruct((species, rows, radial), F32),
        grid=(species, rows // block),
        in_specs=[
            smem,
            pl.BlockSpec((1, block, 2 * radial), lambda s, b: (s, b, 0)),
            pl.BlockSpec((1, 2 * radial, radial), lambda s, b: (s, 0, 0)),
        ],
        out_specs=pl.BlockSpec((1, block, radial), lambda s, b: (s, b, 0)),
        compiler_params=pltpu.CompilerParams(vmem_limit_bytes=16 * 1024 * 1024),
        name="last",
    )(wall_flags, diam.reshape(species, rows, 2 * radial), w)
    return out.reshape(species, angles, planes, radial)


def solution(mesh):
    in_specs = (P(None, "ang", "ax", None), P(), P(), P(), P(), P(), P(None, "ang"), P())
    out_specs = P(None, "ang", "ax", None)
    return jax.shard_map(
        per_device, mesh=mesh, in_specs=in_specs, out_specs=out_specs, check_vma=False
    )
```

```python
import jax
import jax.numpy as jnp
from jax import lax
from jax.experimental import pallas as pl
from jax.experimental.pallas import tpu as pltpu
from jax.sharding import PartitionSpec as P

MESH = pl.DeviceIdType.MESH
F32, BF16 = jnp.float32, jnp.bfloat16
LANES = 128
H = 2
VMEM_LIMIT = 40000000


def comm_kernel(
    conc, courant_in, ang_rate_in, ax_diff_in, rates_in, smap_in, flags_in, rinv,
    d2, w, keep_own,
    courant, ang_rate, ax_diff, rates, smap, flags,
    o0, o1, t0, t1, ob, d1, ma, ml, coef, hxf, pkf, pkb, hx, pa, ha, fl, fl_other, keep_other,
    load_sem, x_send, x_recv, hx_send, hx_recv, a_send, a_recv, fl_sem, m_sem, p_sem,
):
    species, _, planes, radial = o0.shape
    angles = ob.shape[1]
    chunks = angles // (2 * H)
    rows_q = 2 * H
    per_blk = species * rows_q
    ang, ax = lax.axis_index("ang"), lax.axis_index("ax")
    n_ang, n_ax = lax.axis_size("ang"), lax.axis_size("ax")
    opp = lax.rem(ang + n_ang // 2, n_ang)
    up, down = lax.rem(ang + 1, n_ang), lax.rem(ang + n_ang - 1, n_ang)
    has_low, has_high = ax > 0, ax < n_ax - 1
    peer = {"ang": opp, "ax": ax}
    ang_peers = ({"ang": up, "ax": ax}, {"ang": down, "ax": ax})
    ax_peers = ({"ang": opp, "ax": ax + 1}, {"ang": opp, "ax": ax - 1})
    has_to, has_from = (has_high, has_low), (has_low, has_high)
    own, other = (o0, o1), (t0, t1)

    def low(j):
        return j * H

    def high(j):
        return angles - (j + 1) * H

    def angle(j, q):
        return j * H + q if q < H else angles - (j + 1) * H + q - H

    def load(j, end):
        start = (low, high)[end](j)
        return pltpu.make_async_copy(
            conc.at[:, pl.ds(start, H)], o0.at[:, pl.ds(start + 1, H)], load_sem.at[j, end]
        )

    def exchange(j, end):
        start = (low, high)[end](j)
        return pltpu.make_async_remote_copy(
            ob.at[:, pl.ds(start, H)], t0.at[:, pl.ds(start + 1, H)],
            x_send.at[j, end], x_recv.at[j, end], device_id=peer, device_id_type=MESH,
        )

    def ax_copy(step, j, side):
        return pltpu.make_async_remote_copy(
            pkb.at[step, j, side], hx.at[step, j, side],
            hx_send.at[step, j, side], hx_recv.at[step, j, side],
            device_id=ax_peers[side], device_id_type=MESH,
        )

    def ang_copies(step, side):
        t = other[step]
        source, target = ((angles, 0), (1, angles + 1))[side]
        return (
            pltpu.make_async_remote_copy(
                pa.at[step, side], ha.at[step, side],
                a_send.at[step, side, 0], a_recv.at[step, side, 0],
                device_id=ang_peers[side], device_id_type=MESH,
            ),
            pltpu.make_async_remote_copy(
                t.at[:, source], t.at[:, target],
                a_send.at[step, side, 1], a_recv.at[step, side, 1],
                device_id=ang_peers[side], device_id_type=MESH,
            ),
        )

    def flag_copy():
        return pltpu.make_async_remote_copy(
            fl, fl_other, fl_sem.at[0], fl_sem.at[1], device_id=peer, device_id_type=MESH
        )

    small = [
        pltpu.make_async_copy(source, target, p_sem.at[n])
        for n, (source, target) in enumerate((
            (courant_in, courant), (ang_rate_in, ang_rate), (ax_diff_in, ax_diff),
            (rates_in, rates), (smap_in, smap), (flags_in, flags),
        ))
    ]
    for copy in small:
        copy.start()

    @pl.loop(0, chunks)
    def _(j):
        load(j, 0).start()
        load(j, 1).start()

    load_a = pltpu.make_async_copy(rinv.at[:, :radial, :radial], ma, m_sem.at[0])
    load_l = pltpu.make_async_copy(rinv.at[:, radial:, :radial], ml, m_sem.at[1])
    load_a.start()
    load_l.start()

    barrier = pltpu.get_barrier_semaphore()
    for device in (peer, *ang_peers):
        pl.semaphore_signal(barrier, inc=1, device_id=device, device_id_type=MESH)
    for side in range(2):

        @pl.when(has_to[side])
        def _():
            pl.semaphore_signal(barrier, inc=1, device_id=ax_peers[side], device_id_type=MESH)

    for copy in small:
        copy.wait()
    fl[...] = jnp.zeros_like(fl)
    fl[:species, :angles] = flags[...].astype(F32)
    for s in range(species):
        diffusion = ax_diff[s]
        coef[s, 0] = jnp.broadcast_to(
            1.0 - courant[...] - 2.0 * diffusion - 2.0 * ang_rate[s : s + 1], (planes, radial)
        )
        coef[s, 1] = jnp.broadcast_to(courant[...] + diffusion, (planes, radial))
        coef[s, 2] = jnp.broadcast_to(ang_rate[s : s + 1], (planes, radial))
    for side in range(2):

        @pl.when(jnp.logical_not(has_from[side]))
        def _():
            for step in range(2):

                @pl.loop(0, chunks)
                def _(j):
                    hx[step, j, side] = jnp.zeros(hx.shape[3:], BF16)

    gains = []
    for p in range(species):
        gain = jnp.float32(0.0)
        for k in range(rates.shape[0]):
            gain = gain + jnp.where(smap[k, 2] == p, rates[k], jnp.float32(0.0))
        gains.append(gain)

    def cast(j):
        for end in range(2):
            load(j, end).wait()
            start = (low, high)[end](j)
            for i in range(H):
                for s in range(species):
                    ob[s, start + i] = o0[s, start + i + 1].astype(BF16)

    cast(0)
    pl.semaphore_wait(barrier, 3 + jnp.where(has_low, 1, 0) + jnp.where(has_high, 1, 0))
    exchange(0, 0).start()
    exchange(0, 1).start()
    flag_copy().start()

    @pl.loop(1, chunks)
    def _(j):
        cast(j)
        exchange(j, 0).start()
        exchange(j, 1).start()

    load_a.wait()
    load_l.wait()
    flip = (
        lax.broadcasted_iota(jnp.int32, (radial, radial), 0)
        + lax.broadcasted_iota(jnp.int32, (radial, radial), 1)
        == radial - 1
    )
    flip = jnp.where(flip, 1.0, 0.0).astype(BF16)
    for s in range(species):
        w[s, :radial] = ma[s].T
        w[s, radial:] = jnp.dot(ml[s].T, flip, preferred_element_type=F32).astype(BF16)

    flag_copy().wait_recv()
    diagonal = lax.broadcasted_iota(jnp.int32, (angles, LANES), 0) == lax.broadcasted_iota(
        jnp.int32, (angles, LANES), 1
    )
    keep = (keep_own, keep_other)
    for blk, ref in enumerate((fl, fl_other)):
        for s in range(species):
            row = jnp.broadcast_to(ref[s : s + 1], (angles, LANES))
            column = jnp.sum(jnp.where(diagonal, row, 0.0), axis=1, keepdims=True)
            rows = jnp.broadcast_to(1.0 - column, (angles, LANES))
            for a in range(angles):
                keep[blk][s, a] = jnp.broadcast_to(rows[a : a + 1], (planes, LANES))

    lane0 = lax.broadcasted_iota(jnp.int32, (planes, LANES), 1) == 0
    plane = lax.broadcasted_iota(jnp.int32, (planes, LANES), 0)
    first, last = plane == 0, plane == planes - 1

    def forward(step, j):
        for q in range(rows_q):
            a = angle(j, q) + 1
            for blk, ref in ((1, own[step]), (0, other[step])):
                for s in range(species):
                    value = ref[s, a].astype(F32)
                    row = slice(blk * per_blk + s * rows_q + q, blk * per_blk + s * rows_q + q + 1)
                    pkf[0, row, :] = value[planes - 1 : planes]
                    pkf[1, row, :] = value[0:1]

        for side in range(2):
            pkb[step, j, side] = pkf[side].astype(BF16)

            @pl.when(has_to[side])
            def _():
                ax_copy(step, j, side).start()

    def send_edges(step):
        for side in range(2):
            source = (angles, 1)[side]
            for s in range(species):
                pa[step, side, s] = own[step][s, source].astype(BF16)
            for copy in ang_copies(step, side):
                copy.start()

    def take_edges(step):
        for side in range(2):
            for copy in ang_copies(step, side):
                copy.wait_recv()
            target = (0, angles + 1)[side]
            for s in range(species):
                own[step][s, target] = ha[step, side, s].astype(F32)

    def explicit(step, j, store):
        for side in range(2):

            @pl.when(has_from[side])
            def _():
                ax_copy(step, j, side).wait_recv()

            hxf[side] = hx[step, j, side].astype(F32)

        for q in range(rows_q):
            a = angle(j, q) + 1
            for blk, ref in ((0, own[step]), (1, other[step])):
                for lane in range(0, radial, LANES):
                    sl = pl.ds(lane, LANES)
                    f = [ref[s, a, :, sl].astype(F32) for s in range(species)]
                    terms = [
                        gains[s] * (f[(s + 1) % species] * f[(s + 2) % species])
                        for s in range(species)
                    ]
                    total = terms[0] + terms[1] + terms[2]
                    for s in range(species):
                        row = slice(blk * per_blk + s * rows_q + q, blk * per_blk + s * rows_q + q + 1)
                        before = jnp.where(first, hxf[0, row, sl], pltpu.roll(f[s], 1, 0))
                        after = jnp.where(last, hxf[1, row, sl], pltpu.roll(f[s], planes - 1, 0))
                        angular = ref[s, a - 1, :, sl].astype(F32) + ref[s, a + 1, :, sl].astype(F32)
                        value = (
                            coef[s, 0, :, sl] * f[s]
                            + coef[s, 1, :, sl] * before
                            + ax_diff[s] * after
                            + coef[s, 2, :, sl] * angular
                            + (2.0 * terms[s] - total)
                        )
                        store(q, a, blk, s, lane, value.astype(BF16))

    def store_first(q, a, blk, s, lane, value):
        half = rows_q * planes
        sl = pl.ds(lane, LANES)
        offset = q * planes
        d1[s, pl.ds(blk * half + offset, planes), sl] = value
        if blk == 0:
            d1[s, pl.ds(2 * half + offset, planes), sl] = value

    def store_second(q, a, blk, s, lane, value):
        d2[s, a - 1, :, pl.ds(blk * radial + lane, LANES)] = value

    def implicit(j):
        half = rows_q * planes
        for s in range(species):
            y = jnp.dot(d1[s, : 2 * half], w[s, :radial], preferred_element_type=F32)
            y = y + jnp.dot(d1[s, half:], w[s, radial:], preferred_element_type=F32)
            for blk, ref in ((0, o1), (1, t1)):
                for q in range(rows_q):
                    a = angle(j, q)
                    part = y[blk * half + q * planes : blk * half + (q + 1) * planes]
                    head = part[:, :LANES]
                    wall = pltpu.roll(head, LANES - 1, 1) * keep[blk][s, a]
                    ref[s, a + 1, :, :LANES] = jnp.where(lane0, wall, head).astype(ref.dtype)
                    ref[s, a + 1, :, LANES:] = part[:, LANES:].astype(ref.dtype)

    @pl.loop(0, chunks + 2)
    def _(i):
        @pl.when(i < chunks)
        def _():
            exchange(i, 0).wait_recv()
            exchange(i, 1).wait_recv()
            forward(0, i)

            @pl.when(i == 0)
            def _():
                send_edges(0)

        @pl.when(jnp.logical_and(i >= 1, i <= chunks))
        def _():
            @pl.when(i == 1)
            def _():
                take_edges(0)

            explicit(0, i - 1, store_first)
            implicit(i - 1)
            forward(1, i - 1)

            @pl.when(i == 1)
            def _():
                send_edges(1)

        @pl.when(i >= 2)
        def _():
            @pl.when(i == 2)
            def _():
                take_edges(1)

            explicit(1, i - 2, store_second)

    flag_copy().wait_send()
    for step in range(2):
        for side in range(2):
            for copy in ang_copies(step, side):
                copy.wait_send()

    @pl.loop(0, chunks)
    def _(j):
        for end in range(2):
            exchange(j, end).wait_send()
        for step in range(2):
            for side in range(2):

                @pl.when(has_to[side])
                def _():
                    ax_copy(step, j, side).wait_send()


def final_kernel(diam, w, keep, out):
    planes = keep.shape[2]
    s, block = pl.program_id(0), pl.program_id(1)
    rows = out.shape[1]
    count = rows // planes
    y = jnp.dot(
        diam[s, pl.ds(pl.multiple_of(block * rows, rows), rows)], w[s], preferred_element_type=F32
    )
    out[0] = y
    lane0 = lax.broadcasted_iota(jnp.int32, (planes, LANES), 1) == 0
    for i in range(count):
        head = y[i * planes : (i + 1) * planes, :LANES]
        wall = pltpu.roll(head, LANES - 1, 1) * keep[s, block * count + i]
        out[0, pl.ds(i * planes, planes), :LANES] = jnp.where(lane0, wall, head)


def per_device(
    concentration, courant, axial_diffusion, angular_rate, rate_constants, species_map, wall_flags, radial_inverse
):
    species, angles, planes, radial = concentration.shape
    chunks, rows_q = angles // (2 * H), 2 * H
    packed = 2 * species * rows_q
    vmem = pl.BlockSpec(memory_space=pltpu.VMEM)
    hbm = pl.BlockSpec(memory_space=pltpu.HBM)
    dma = pltpu.SemaphoreType.DMA
    diam, w, keep = pl.pallas_call(
        comm_kernel,
        out_shape=(
            pltpu.VMEM((species, angles, planes, 2 * radial), BF16),
            pltpu.VMEM((species, 2 * radial, radial), BF16),
            pltpu.VMEM((species, angles, planes, LANES), F32),
        ),
        in_specs=[hbm] * 8,
        out_specs=(vmem, vmem, vmem),
        scratch_shapes=[
            pltpu.VMEM((1, radial), F32),
            pltpu.VMEM((species, radial), F32),
            pltpu.SMEM(axial_diffusion.shape, F32),
            pltpu.SMEM(rate_constants.shape, F32),
            pltpu.SMEM(species_map.shape, jnp.int32),
            pltpu.VMEM((species, angles), jnp.int32),
            pltpu.VMEM((species, angles + 2, planes, radial), F32),
            pltpu.VMEM((species, angles + 2, planes, radial), F32),
            pltpu.VMEM((species, angles + 2, planes, radial), BF16),
            pltpu.VMEM((species, angles + 2, planes, radial), BF16),
            pltpu.VMEM((species, angles, planes, radial), BF16),
            pltpu.VMEM((species, 3 * rows_q * planes, radial), BF16),
            pltpu.VMEM((species, radial, radial), BF16),
            pltpu.VMEM((species, radial, radial), BF16),
            pltpu.VMEM((species, 3, planes, radial), F32),
            pltpu.VMEM((2, packed, radial), F32),
            pltpu.VMEM((2, packed, radial), F32),
            pltpu.VMEM((2, chunks, 2, packed, radial), BF16),
            pltpu.VMEM((2, chunks, 2, packed, radial), BF16),
            pltpu.VMEM((2, 2, species, planes, radial), BF16),
            pltpu.VMEM((2, 2, species, planes, radial), BF16),
            pltpu.VMEM((8, LANES), F32),
            pltpu.VMEM((8, LANES), F32),
            pltpu.VMEM((species, angles, planes, LANES), F32),
            dma((chunks, 2)),
            dma((chunks, 2)),
            dma((chunks, 2)),
            dma((2, chunks, 2)),
            dma((2, chunks, 2)),
            dma((2, 2, 2)),
            dma((2, 2, 2)),
            dma((2,)),
            dma((2,)),
            dma((6,)),
        ],
        compiler_params=pltpu.CompilerParams(
            collective_id=0, has_side_effects=True, vmem_limit_bytes=VMEM_LIMIT
        ),
        name="steps",
    )(
        *(
            pltpu.with_memory_space_constraint(x, pltpu.HBM)
            for x in (
                concentration, courant.reshape(1, radial), angular_rate, axial_diffusion,
                rate_constants, species_map, wall_flags, radial_inverse,
            )
        )
    )
    rows = angles * planes
    block = min(rows, 256)
    out = pl.pallas_call(
        final_kernel,
        out_shape=jax.ShapeDtypeStruct((species, rows, radial), F32),
        grid=(species, rows // block),
        in_specs=[vmem, vmem, vmem],
        out_specs=pl.BlockSpec((1, block, radial), lambda s, b: (s, b, 0)),
        compiler_params=pltpu.CompilerParams(vmem_limit_bytes=16 * 1024 * 1024),
        name="last",
    )(diam.reshape(species, rows, 2 * radial), w, keep)
    return out.reshape(species, angles, planes, radial)


def solution(mesh):
    in_specs = (P(None, "ang", "ax", None), P(), P(), P(), P(), P(), P(None, "ang"), P())
    out_specs = P(None, "ang", "ax", None)
    return jax.shard_map(
        per_device, mesh=mesh, in_specs=in_specs, out_specs=out_specs, check_vma=False
    )
```

```python
import jax
import jax.numpy as jnp
from jax import lax
from jax.experimental import pallas as pl
from jax.experimental.pallas import tpu as pltpu
from jax.sharding import PartitionSpec as P

MESH = pl.DeviceIdType.MESH
F32, BF16 = jnp.float32, jnp.bfloat16
LANES = 128
H = 2
DIRECT = 3
VMEM_LIMIT = 40000000


def comm_kernel(
    conc, courant_in, ang_rate_in, ax_diff_in, rates_in, smap_in, flags_in, rinv,
    out,
    courant, ang_rate, ax_diff, rates, smap, flags,
    o0, o1, t0, t1, ob, d1, d2, w, ma, ml, coef, hxf, pkf, pko, pkt, pk1, hx0, hx1, pa, ha, fl, fl_other, keep,
    load_sem, x_send, x_recv, hxt_send, hxe_send, hx0_recv, hx1_send, hx1_recv, a_send, a_recv, fl_sem, m_sem, p_sem,
):
    species, _, planes, radial = o0.shape
    angles = ob.shape[1]
    chunks = angles // (2 * H)
    rows_q = 2 * H
    per_blk = species * rows_q
    forwarded = chunks - DIRECT
    ang, ax = lax.axis_index("ang"), lax.axis_index("ax")
    n_ang, n_ax = lax.axis_size("ang"), lax.axis_size("ax")
    opp = lax.rem(ang + n_ang // 2, n_ang)
    up, down = lax.rem(ang + 1, n_ang), lax.rem(ang + n_ang - 1, n_ang)
    has_low, has_high = ax > 0, ax < n_ax - 1
    peer = {"ang": opp, "ax": ax}
    ang_peers = ({"ang": up, "ax": ax}, {"ang": down, "ax": ax})
    ax_peers = ({"ang": opp, "ax": ax + 1}, {"ang": opp, "ax": ax - 1})
    ax_own = ({"ang": ang, "ax": ax + 1}, {"ang": ang, "ax": ax - 1})
    has_to, has_from = (has_high, has_low), (has_low, has_high)
    own, other = (o0, o1), (t0, t1)

    def angle(j, q):
        return j * H + q if q < H else angles - (j + 1) * H + q - H

    def remote(source, target, send, recv, device):
        return pltpu.make_async_remote_copy(
            source, target, send, recv, device_id=device, device_id_type=MESH
        )

    def load(j, end):
        start = (j * H, angles - (j + 1) * H)[end]
        return pltpu.make_async_copy(
            conc.at[:, pl.ds(start, H)], o0.at[:, pl.ds(start + 1, H)], load_sem.at[j, end]
        )

    def exchange(j, end, count):
        first = j * H + (0 if count > H else 1)
        start = (first, angles - first - count)[end]
        return remote(
            ob.at[:, pl.ds(start, count)], t0.at[:, pl.ds(start + 1, count)],
            x_send.at[j, end], x_recv.at[j, end], peer,
        )

    def each_exchange(i, act):
        for cond, count in ((i == 0, H + 1), ((i > 0) & (i < chunks - 1), H), (i == chunks - 1, H - 1)):

            @pl.when(cond)
            def _():
                act(exchange(i, 0, count))
                act(exchange(i, 1, count))

    def other_copy(j, side):
        return remote(
            pko.at[j, side], hx0.at[j, side, 1], hxt_send.at[j, side], hx0_recv.at[j, side, 1], ax_peers[side]
        )

    def own_copy(j, side, direct):
        return remote(
            (pko if direct else pkt).at[j, side], hx0.at[j, side, 0],
            hxe_send.at[j, side], hx0_recv.at[j, side, 0], (ax_own if direct else ax_peers)[side],
        )

    def second_copy(j, side):
        return remote(
            pk1.at[j, side], hx1.at[j, side], hx1_send.at[j, side], hx1_recv.at[j, side], ax_peers[side]
        )

    def ang_copies(step, side):
        t = other[step]
        source, target = ((angles, 0), (1, angles + 1))[side]
        return (
            remote(pa.at[step, side], ha.at[step, side], a_send.at[step, side, 0], a_recv.at[step, side, 0], ang_peers[side]),
            remote(t.at[:, source], t.at[:, target], a_send.at[step, side, 1], a_recv.at[step, side, 1], ang_peers[side]),
        )

    def flag_copy():
        return remote(fl, fl_other, fl_sem.at[0], fl_sem.at[1], peer)

    barrier = pltpu.get_barrier_semaphore()
    for device in (peer, *ang_peers):
        pl.semaphore_signal(barrier, inc=1, device_id=device, device_id_type=MESH)
    for side in range(2):

        @pl.when(has_to[side])
        def _():
            pl.semaphore_signal(barrier, inc=1, device_id=ax_peers[side], device_id_type=MESH)
            pl.semaphore_signal(barrier, inc=1, device_id=ax_own[side], device_id_type=MESH)

    for j in range(chunks):
        load(j, 0).start()
        load(j, 1).start()
    small = [
        pltpu.make_async_copy(source, target, p_sem.at[n])
        for n, (source, target) in enumerate((
            (courant_in, courant), (ang_rate_in, ang_rate), (ax_diff_in, ax_diff),
            (rates_in, rates), (smap_in, smap), (flags_in, flags),
        ))
    ]
    for copy in small:
        copy.start()
    load_a = pltpu.make_async_copy(rinv.at[:, :radial, :radial], ma, m_sem.at[0])
    load_l = pltpu.make_async_copy(rinv.at[:, radial:, :radial], ml, m_sem.at[1])
    load_a.start()
    load_l.start()

    def cast(j):
        for end in range(2):
            load(j, end).wait()
            start = (j * H, angles - (j + 1) * H)[end]
            for i in range(H):
                for s in range(species):
                    ob[s, start + i] = o0[s, start + i + 1].astype(BF16)

    cast(0)
    cast(1)
    for copy in small:
        copy.wait()
    fl[...] = jnp.zeros_like(fl)
    fl[:species, :angles] = flags[...].astype(F32)
    pl.semaphore_wait(barrier, 3 + jnp.where(has_low, 2, 0) + jnp.where(has_high, 2, 0))
    def pack(target, ref, j, per):
        for q in range(rows_q):
            a = angle(j, q) + 1
            for s in range(species):
                value = ref[s, a].astype(F32)
                row = slice(s * rows_q + q, s * rows_q + q + 1)
                pkf[per, 0, row, :] = value[planes - 1 : planes]
                pkf[per, 1, row, :] = value[0:1]
        for side in range(2):
            target(side)[...] = pkf[per, side].astype(BF16)

    def send(j):
        count = H + 1 if j == 0 else H if j < chunks - 1 else H - 1
        exchange(j, 0, count).start()
        exchange(j, 1, count).start()

    def send_planes(j, direct):
        pack(lambda side: pko.at[j, side], o0, j, 0)
        for side in range(2):

            @pl.when(has_to[side])
            def _():
                other_copy(j, side).start()
                if direct:
                    own_copy(j, side, True).start()

    flag_copy().start()
    send(0)
    for j in range(2, chunks):
        cast(j)
    for j in range(forwarded, chunks):
        send_planes(j, True)
    for j in range(1, chunks):
        send(j)

    @pl.loop(0, forwarded)
    def _(j):
        send_planes(j, False)

    for s in range(species):
        diffusion = ax_diff[s]
        coef[s, 0] = jnp.broadcast_to(
            1.0 - courant[...] - 2.0 * diffusion - 2.0 * ang_rate[s : s + 1], (planes, radial)
        )
        coef[s, 1] = jnp.broadcast_to(courant[...] + diffusion, (planes, radial))
        coef[s, 2] = jnp.broadcast_to(ang_rate[s : s + 1], (planes, radial))
    for side in range(2):

        @pl.when(jnp.logical_not(has_from[side]))
        def _():
            @pl.loop(0, chunks)
            def _(j):
                hx0[j, side] = jnp.zeros(hx0.shape[2:], BF16)
                hx1[j, side] = jnp.zeros(hx1.shape[2:], BF16)

    gains = []
    for p in range(species):
        gain = jnp.float32(0.0)
        for k in range(rates.shape[0]):
            gain = gain + jnp.where(smap[k, 2] == p, rates[k], jnp.float32(0.0))
        gains.append(gain)

    load_a.wait()
    load_l.wait()
    flip = (
        lax.broadcasted_iota(jnp.int32, (radial, radial), 0)
        + lax.broadcasted_iota(jnp.int32, (radial, radial), 1)
        == radial - 1
    )
    flip = jnp.where(flip, 1.0, 0.0).astype(BF16)
    for s in range(species):
        w[s, :radial] = ma[s].T
        w[s, radial:] = jnp.dot(ml[s].T, flip, preferred_element_type=F32).astype(BF16)

    flag_copy().wait_recv()
    diagonal = lax.broadcasted_iota(jnp.int32, (angles, LANES), 0) == lax.broadcasted_iota(
        jnp.int32, (angles, LANES), 1
    )
    for blk, ref in enumerate((fl, fl_other)):
        for s in range(species):
            row = jnp.broadcast_to(ref[s : s + 1], (angles, LANES))
            column = jnp.sum(jnp.where(diagonal, row, 0.0), axis=1, keepdims=True)
            rows = jnp.broadcast_to(1.0 - column, (angles, LANES))
            for a in range(angles):
                keep[blk, s, a] = jnp.broadcast_to(rows[a : a + 1], (planes, LANES))

    lane0 = lax.broadcasted_iota(jnp.int32, (planes, LANES), 1) == 0
    plane = lax.broadcasted_iota(jnp.int32, (planes, LANES), 0)
    first, last = plane == 0, plane == planes - 1
    half = rows_q * planes

    def send_edges(step):
        for side in range(2):
            source = (angles, 1)[side]
            for s in range(species):
                pa[step, side, s] = own[step][s, source].astype(BF16)
            for copy in ang_copies(step, side):
                copy.start()

    def take_edges(step):
        for side in range(2):
            for copy in ang_copies(step, side):
                copy.wait_recv()
            target = (0, angles + 1)[side]
            for s in range(species):
                own[step][s, target] = ha[step, side, s].astype(F32)

    def explicit(step, j):
        for side in range(2):

            @pl.when(has_from[side])
            def _():
                if step:
                    second_copy(j, side).wait_recv()
                else:
                    own_copy(j, side, True).wait_recv()
                    other_copy(j, side).wait_recv()

            for blk in range(2):
                hxf[side, blk] = (hx0, hx1)[step][j, side, blk].astype(F32)
        for q in range(rows_q):
            a = angle(j, q) + 1
            for blk, ref in ((0, own[step]), (1, other[step])):
                for lane in range(0, radial, LANES):
                    sl = pl.ds(lane, LANES)
                    f = [ref[s, a, :, sl].astype(F32) for s in range(species)]
                    terms = [
                        gains[s] * (f[(s + 1) % species] * f[(s + 2) % species])
                        for s in range(species)
                    ]
                    total = terms[0] + terms[1] + terms[2]
                    for s in range(species):
                        row = slice(s * rows_q + q, s * rows_q + q + 1)
                        before = jnp.where(first, hxf[0, blk, row, sl], pltpu.roll(f[s], 1, 0))
                        after = jnp.where(last, hxf[1, blk, row, sl], pltpu.roll(f[s], planes - 1, 0))
                        angular = ref[s, a - 1, :, sl].astype(F32) + ref[s, a + 1, :, sl].astype(F32)
                        value = (
                            coef[s, 0, :, sl] * f[s]
                            + coef[s, 1, :, sl] * before
                            + ax_diff[s] * after
                            + coef[s, 2, :, sl] * angular
                            + (2.0 * terms[s] - total)
                        ).astype(BF16)
                        rows = pl.ds(q * planes, planes)
                        if step:
                            d2[s, blk, lax.rem(j, 2), rows, sl] = value
                        else:
                            d1[s, blk, rows, sl] = value
                            if blk == 0:
                                d1[s, 2, rows, sl] = value

    def walled(ref, s, a, blk, part, offset):
        head = part[:, :LANES]
        wall = pltpu.roll(head, LANES - 1, 1) * keep[blk, s, a]
        ref[s, a + offset, :, :LANES] = jnp.where(lane0, wall, head).astype(ref.dtype)
        ref[s, a + offset, :, LANES:] = part[:, LANES:].astype(ref.dtype)

    def implicit_first(j):
        for s in range(species):
            mine = d1[s, :2].reshape(2 * half, radial)
            theirs = d1[s, 1:].reshape(2 * half, radial)
            y = jnp.dot(mine, w[s, :radial], preferred_element_type=F32)
            y = y + jnp.dot(theirs, w[s, radial:], preferred_element_type=F32)
            for blk, ref in ((0, o1), (1, t1)):
                for q in range(rows_q):
                    part = y[blk * half + q * planes : blk * half + (q + 1) * planes]
                    walled(ref, s, angle(j, q), blk, part, 1)

    def implicit_second(j):
        for s in range(species):
            y = jnp.dot(d2[s, 0].reshape(2 * half, radial), w[s, :radial], preferred_element_type=F32)
            y = y + jnp.dot(d2[s, 1].reshape(2 * half, radial), w[s, radial:], preferred_element_type=F32)
            for c in range(2):
                for q in range(rows_q):
                    part = y[c * half + q * planes : c * half + (q + 1) * planes]
                    walled(out, s, angle(j - 1 + c, q), 0, part, 0)

    def second_step(j):
        @pl.when(j == 0)
        def _():
            take_edges(1)

        explicit(1, j)

        @pl.when(lax.rem(j, 2) == 1)
        def _():
            implicit_second(j)

    inside = max(chunks - 4, 0)

    @pl.loop(0, chunks + 1)
    def _(i):
        @pl.when(i < forwarded)
        def _():
            each_exchange(i, lambda copy: copy.wait_recv())
            pack(lambda side: pkt.at[i, side], t0, i, 0)
            for side in range(2):

                @pl.when(has_to[side])
                def _():
                    own_copy(i, side, False).start()

            @pl.when(i == 0)
            def _():
                send_edges(0)

        if inside:

            @pl.when((i >= 3) & (i < 3 + inside))
            def _():
                second_step(i - 3)

        @pl.when(i >= 1)
        def _():
            @pl.when(i - 1 >= forwarded)
            def _():
                each_exchange(i - 1, lambda copy: copy.wait_recv())

            @pl.when(i == 1)
            def _():
                take_edges(0)

            explicit(0, i - 1)
            implicit_first(i - 1)
            pack(lambda side: pk1.at[i - 1, side, 1], o1, i - 1, 0)
            pack(lambda side: pk1.at[i - 1, side, 0], t1, i - 1, 1)
            for side in range(2):

                @pl.when(has_to[side])
                def _():
                    second_copy(i - 1, side).start()

            @pl.when(i == 1)
            def _():
                send_edges(1)

    @pl.loop(inside, chunks)
    def _(j):
        second_step(j)

    flag_copy().wait_send()
    for step in range(2):
        for side in range(2):
            for copy in ang_copies(step, side):
                copy.wait_send()

    @pl.loop(0, chunks)
    def _(j):
        each_exchange(j, lambda copy: copy.wait_send())
        for side in range(2):

            @pl.when(has_to[side])
            def _():
                other_copy(j, side).wait_send()
                own_copy(j, side, True).wait_send()
                second_copy(j, side).wait_send()


def per_device(
    concentration, courant, axial_diffusion, angular_rate, rate_constants, species_map, wall_flags, radial_inverse
):
    species, angles, planes, radial = concentration.shape
    chunks, rows_q = angles // (2 * H), 2 * H
    packed, half = species * rows_q, rows_q * planes
    hbm, vmem = pl.BlockSpec(memory_space=pltpu.HBM), pl.BlockSpec(memory_space=pltpu.VMEM)
    dma = pltpu.SemaphoreType.DMA
    return pl.pallas_call(
        comm_kernel,
        out_shape=pltpu.VMEM((species, angles, planes, radial), F32),
        in_specs=[hbm] * 8,
        out_specs=vmem,
        scratch_shapes=[
            pltpu.VMEM((1, radial), F32),
            pltpu.VMEM((species, radial), F32),
            pltpu.SMEM(axial_diffusion.shape, F32),
            pltpu.SMEM(rate_constants.shape, F32),
            pltpu.SMEM(species_map.shape, jnp.int32),
            pltpu.VMEM((species, angles), jnp.int32),
            pltpu.VMEM((species, angles + 2, planes, radial), F32),
            pltpu.VMEM((species, angles + 2, planes, radial), F32),
            pltpu.VMEM((species, angles + 2, planes, radial), BF16),
            pltpu.VMEM((species, angles + 2, planes, radial), BF16),
            pltpu.VMEM((species, angles, planes, radial), BF16),
            pltpu.VMEM((species, 3, half, radial), BF16),
            pltpu.VMEM((species, 2, 2, half, radial), BF16),
            pltpu.VMEM((species, 2 * radial, radial), BF16),
            pltpu.VMEM((species, radial, radial), BF16),
            pltpu.VMEM((species, radial, radial), BF16),
            pltpu.VMEM((species, 3, planes, radial), F32),
            pltpu.VMEM((2, 2, packed, radial), F32),
            pltpu.VMEM((2, 2, packed, radial), F32),
            pltpu.VMEM((chunks, 2, packed, radial), BF16),
            pltpu.VMEM((chunks, 2, packed, radial), BF16),
            pltpu.VMEM((chunks, 2, 2, packed, radial), BF16),
            pltpu.VMEM((chunks, 2, 2, packed, radial), BF16),
            pltpu.VMEM((chunks, 2, 2, packed, radial), BF16),
            pltpu.VMEM((2, 2, species, planes, radial), BF16),
            pltpu.VMEM((2, 2, species, planes, radial), BF16),
            pltpu.VMEM((8, LANES), F32),
            pltpu.VMEM((8, LANES), F32),
            pltpu.VMEM((2, species, angles, planes, LANES), F32),
            dma((chunks, 2)),
            dma((chunks, 2)),
            dma((chunks, 2)),
            dma((chunks, 2)),
            dma((chunks, 2)),
            dma((chunks, 2, 2)),
            dma((chunks, 2)),
            dma((chunks, 2)),
            dma((2, 2, 2)),
            dma((2, 2, 2)),
            dma((2,)),
            dma((2,)),
            dma((6,)),
        ],
        compiler_params=pltpu.CompilerParams(
            collective_id=0, has_side_effects=True, vmem_limit_bytes=VMEM_LIMIT
        ),
        name="steps",
    )(
        *(
            pltpu.with_memory_space_constraint(x, pltpu.HBM)
            for x in (
                concentration, courant.reshape(1, radial), angular_rate, axial_diffusion,
                rate_constants, species_map, wall_flags, radial_inverse,
            )
        )
    )


def solution(mesh):
    in_specs = (P(None, "ang", "ax", None), P(), P(), P(), P(), P(), P(None, "ang"), P())
    out_specs = P(None, "ang", "ax", None)
    return jax.shard_map(
        per_device, mesh=mesh, in_specs=in_specs, out_specs=out_specs, check_vma=False
    )
```

```python
import jax
import jax.numpy as jnp
from jax import lax
from jax.experimental import pallas as pl
from jax.experimental.pallas import tpu as pltpu
from jax.sharding import PartitionSpec as P

MESH = pl.DeviceIdType.MESH
F32, BF16 = jnp.float32, jnp.bfloat16
LANES = 128
H = 2
DIRECT = 3
VMEM_LIMIT = 40000000


def comm_kernel(
    conc, courant_in, ang_rate_in, ax_diff_in, rates_in, smap_in, flags_in, rinv,
    out,
    courant, ang_rate, ax_diff, rates, smap, flags,
    o0, o1, t0, t1, ob, d1, d2, w, ma, ml, coef, hxf, pkf, pko, pkt, pk1, hx0, hx1, pa, ha, fl, fl_other, keep,
    load_sem, x_send, x_recv, hxt_send, hxe_send, hx0_recv, hx1_send, hx1_recv, a_send, a_recv, fl_sem, m_sem, p_sem,
):
    species, _, planes, radial = o0.shape
    angles = ob.shape[1]
    chunks = angles // (2 * H)
    rows_q = 2 * H
    per_blk = species * rows_q
    forwarded = chunks - DIRECT
    ang, ax = lax.axis_index("ang"), lax.axis_index("ax")
    n_ang, n_ax = lax.axis_size("ang"), lax.axis_size("ax")
    opp = lax.rem(ang + n_ang // 2, n_ang)
    side_count = n_ang // 2
    place = lax.rem(ang, side_count)
    base = ang - place
    up = base + lax.rem(place + 1, side_count)
    down = base + lax.rem(place + side_count - 1, side_count)
    wraps = (place == side_count - 1, place == 0)
    has_low, has_high = ax > 0, ax < n_ax - 1
    peer = {"ang": opp, "ax": ax}
    ang_peers = ({"ang": up, "ax": ax}, {"ang": down, "ax": ax})
    ax_peers = ({"ang": opp, "ax": ax + 1}, {"ang": opp, "ax": ax - 1})
    ax_own = ({"ang": ang, "ax": ax + 1}, {"ang": ang, "ax": ax - 1})
    has_to, has_from = (has_high, has_low), (has_low, has_high)
    own, other = (o0, o1), (t0, t1)

    def angle(j, q):
        return j * H + q if q < H else angles - (j + 1) * H + q - H

    def remote(source, target, send, recv, device):
        return pltpu.make_async_remote_copy(
            source, target, send, recv, device_id=device, device_id_type=MESH
        )

    def load(j, end):
        start = (j * H, angles - (j + 1) * H)[end]
        return pltpu.make_async_copy(
            conc.at[:, pl.ds(start, H)], o0.at[:, pl.ds(start + 1, H)], load_sem.at[j, end]
        )

    def exchange(j, end, count):
        first = j * H + (0 if count > H else 1)
        start = (first, angles - first - count)[end]
        return remote(
            ob.at[:, pl.ds(start, count)], t0.at[:, pl.ds(start + 1, count)],
            x_send.at[j, end], x_recv.at[j, end], peer,
        )

    def each_exchange(i, act):
        for cond, count in ((i == 0, H + 1), ((i > 0) & (i < chunks - 1), H), (i == chunks - 1, H - 1)):

            @pl.when(cond)
            def _():
                act(exchange(i, 0, count))
                act(exchange(i, 1, count))

    def other_copy(j, side):
        return remote(
            pko.at[j, side], hx0.at[j, side, 1], hxt_send.at[j, side], hx0_recv.at[j, side, 1], ax_peers[side]
        )

    def own_copy(j, side, direct):
        return remote(
            (pko if direct else pkt).at[j, side], hx0.at[j, side, 0],
            hxe_send.at[j, side], hx0_recv.at[j, side, 0], (ax_own if direct else ax_peers)[side],
        )

    def second_copy(j, side):
        return remote(
            pk1.at[j, side], hx1.at[j, side], hx1_send.at[j, side], hx1_recv.at[j, side], ax_peers[side]
        )

    def ang_copies(step, side, swapped=0):
        t = other[step]
        source, target = ((angles, 0), (1, angles + 1))[side]
        targets = (ha.at[step, side], t.at[:, target])
        return tuple(
            remote(
                start, targets[n ^ swapped], a_send.at[step, side, n], a_recv.at[step, side, n ^ swapped], ang_peers[side]
            )
            for n, start in enumerate((pa.at[step, side], t.at[:, source]))
        )

    def flag_copy():
        return remote(fl, fl_other, fl_sem.at[0], fl_sem.at[1], peer)

    barrier = pltpu.get_barrier_semaphore()
    for device in (peer, *ang_peers):
        pl.semaphore_signal(barrier, inc=1, device_id=device, device_id_type=MESH)
    for side in range(2):

        @pl.when(has_to[side])
        def _():
            pl.semaphore_signal(barrier, inc=1, device_id=ax_peers[side], device_id_type=MESH)
            pl.semaphore_signal(barrier, inc=1, device_id=ax_own[side], device_id_type=MESH)

    for j in range(chunks):
        load(j, 0).start()
        load(j, 1).start()
    small = [
        pltpu.make_async_copy(source, target, p_sem.at[n])
        for n, (source, target) in enumerate((
            (courant_in, courant), (ang_rate_in, ang_rate), (ax_diff_in, ax_diff),
            (rates_in, rates), (smap_in, smap), (flags_in, flags),
        ))
    ]
    for copy in small:
        copy.start()
    load_a = pltpu.make_async_copy(rinv.at[:, :radial, :radial], ma, m_sem.at[0])
    load_l = pltpu.make_async_copy(rinv.at[:, radial:, :radial], ml, m_sem.at[1])
    load_a.start()
    load_l.start()

    def cast(j):
        for end in range(2):
            load(j, end).wait()
            start = (j * H, angles - (j + 1) * H)[end]
            for i in range(H):
                for s in range(species):
                    ob[s, start + i] = o0[s, start + i + 1].astype(BF16)

    cast(0)
    cast(1)
    for copy in small:
        copy.wait()
    fl[...] = jnp.zeros_like(fl)
    fl[:species, :angles] = flags[...].astype(F32)
    pl.semaphore_wait(barrier, 3 + jnp.where(has_low, 2, 0) + jnp.where(has_high, 2, 0))
    def pack(target, ref, j, per):
        for q in range(rows_q):
            a = angle(j, q) + 1
            for s in range(species):
                value = ref[s, a].astype(F32)
                row = slice(s * rows_q + q, s * rows_q + q + 1)
                pkf[per, 0, row, :] = value[planes - 1 : planes]
                pkf[per, 1, row, :] = value[0:1]
        for side in range(2):
            target(side)[...] = pkf[per, side].astype(BF16)

    def send(j):
        count = H + 1 if j == 0 else H if j < chunks - 1 else H - 1
        exchange(j, 0, count).start()
        exchange(j, 1, count).start()

    def send_planes(j, direct):
        pack(lambda side: pko.at[j, side], o0, j, 0)
        for side in range(2):

            @pl.when(has_to[side])
            def _():
                other_copy(j, side).start()
                if direct:
                    own_copy(j, side, True).start()

    flag_copy().start()
    send(0)
    for j in range(2, chunks):
        cast(j)
    for j in range(forwarded, chunks):
        send_planes(j, True)
    for j in range(1, chunks):
        send(j)

    @pl.loop(0, forwarded)
    def _(j):
        send_planes(j, False)

    for s in range(species):
        diffusion = ax_diff[s]
        coef[s, 0] = jnp.broadcast_to(
            1.0 - courant[...] - 2.0 * diffusion - 2.0 * ang_rate[s : s + 1], (planes, radial)
        )
        coef[s, 1] = jnp.broadcast_to(courant[...] + diffusion, (planes, radial))
        coef[s, 2] = jnp.broadcast_to(ang_rate[s : s + 1], (planes, radial))
    for side in range(2):

        @pl.when(jnp.logical_not(has_from[side]))
        def _():
            @pl.loop(0, chunks)
            def _(j):
                hx0[j, side] = jnp.zeros(hx0.shape[2:], BF16)
                hx1[j, side] = jnp.zeros(hx1.shape[2:], BF16)

    gains = []
    for p in range(species):
        gain = jnp.float32(0.0)
        for k in range(rates.shape[0]):
            gain = gain + jnp.where(smap[k, 2] == p, rates[k], jnp.float32(0.0))
        gains.append(gain)

    load_a.wait()
    load_l.wait()
    flip = (
        lax.broadcasted_iota(jnp.int32, (radial, radial), 0)
        + lax.broadcasted_iota(jnp.int32, (radial, radial), 1)
        == radial - 1
    )
    flip = jnp.where(flip, 1.0, 0.0).astype(BF16)
    for s in range(species):
        w[s, :radial] = ma[s].T
        w[s, radial:] = jnp.dot(ml[s].T, flip, preferred_element_type=F32).astype(BF16)

    flag_copy().wait_recv()
    diagonal = lax.broadcasted_iota(jnp.int32, (angles, LANES), 0) == lax.broadcasted_iota(
        jnp.int32, (angles, LANES), 1
    )
    for blk, ref in enumerate((fl, fl_other)):
        for s in range(species):
            row = jnp.broadcast_to(ref[s : s + 1], (angles, LANES))
            column = jnp.sum(jnp.where(diagonal, row, 0.0), axis=1, keepdims=True)
            rows = jnp.broadcast_to(1.0 - column, (angles, LANES))
            for a in range(angles):
                keep[blk, s, a] = jnp.broadcast_to(rows[a : a + 1], (planes, LANES))

    lane0 = lax.broadcasted_iota(jnp.int32, (planes, LANES), 1) == 0
    plane = lax.broadcasted_iota(jnp.int32, (planes, LANES), 0)
    first, last = plane == 0, plane == planes - 1
    half = rows_q * planes

    def send_edges(step):
        for side in range(2):
            source = (angles, 1)[side]
            for s in range(species):
                pa[step, side, s] = own[step][s, source].astype(BF16)
            for swapped in range(2):

                @pl.when(wraps[side] if swapped else jnp.logical_not(wraps[side]))
                def _():
                    for copy in ang_copies(step, side, swapped):
                        copy.start()

    def take_edges(step):
        for side in range(2):
            for copy in ang_copies(step, side):
                copy.wait_recv()
            target = (0, angles + 1)[side]
            for s in range(species):
                own[step][s, target] = ha[step, side, s].astype(F32)

    def explicit(step, j):
        for side in range(2):

            @pl.when(has_from[side])
            def _():
                if step:
                    second_copy(j, side).wait_recv()
                else:
                    own_copy(j, side, True).wait_recv()
                    other_copy(j, side).wait_recv()

            for blk in range(2):
                hxf[side, blk] = (hx0, hx1)[step][j, side, blk].astype(F32)
        for q in range(rows_q):
            a = angle(j, q) + 1
            for blk, ref in ((0, own[step]), (1, other[step])):
                for lane in range(0, radial, LANES):
                    sl = pl.ds(lane, LANES)
                    f = [ref[s, a, :, sl].astype(F32) for s in range(species)]
                    terms = [
                        gains[s] * (f[(s + 1) % species] * f[(s + 2) % species])
                        for s in range(species)
                    ]
                    total = terms[0] + terms[1] + terms[2]
                    for s in range(species):
                        row = slice(s * rows_q + q, s * rows_q + q + 1)
                        before = jnp.where(first, hxf[0, blk, row, sl], pltpu.roll(f[s], 1, 0))
                        after = jnp.where(last, hxf[1, blk, row, sl], pltpu.roll(f[s], planes - 1, 0))
                        angular = ref[s, a - 1, :, sl].astype(F32) + ref[s, a + 1, :, sl].astype(F32)
                        value = (
                            coef[s, 0, :, sl] * f[s]
                            + coef[s, 1, :, sl] * before
                            + ax_diff[s] * after
                            + coef[s, 2, :, sl] * angular
                            + (2.0 * terms[s] - total)
                        ).astype(BF16)
                        rows = pl.ds(q * planes, planes)
                        if step:
                            d2[s, blk, lax.rem(j, 2), rows, sl] = value
                        else:
                            d1[s, blk, rows, sl] = value
                            if blk == 0:
                                d1[s, 2, rows, sl] = value

    def walled(ref, s, a, blk, part, offset):
        head = part[:, :LANES]
        wall = pltpu.roll(head, LANES - 1, 1) * keep[blk, s, a]
        ref[s, a + offset, :, :LANES] = jnp.where(lane0, wall, head).astype(ref.dtype)
        ref[s, a + offset, :, LANES:] = part[:, LANES:].astype(ref.dtype)

    def implicit_first(j):
        for s in range(species):
            mine = d1[s, :2].reshape(2 * half, radial)
            theirs = d1[s, 1:].reshape(2 * half, radial)
            y = jnp.dot(mine, w[s, :radial], preferred_element_type=F32)
            y = y + jnp.dot(theirs, w[s, radial:], preferred_element_type=F32)
            for blk, ref in ((0, o1), (1, t1)):
                for q in range(rows_q):
                    part = y[blk * half + q * planes : blk * half + (q + 1) * planes]
                    walled(ref, s, angle(j, q), blk, part, 1)

    def implicit_second(j):
        for s in range(species):
            y = jnp.dot(d2[s, 0].reshape(2 * half, radial), w[s, :radial], preferred_element_type=F32)
            y = y + jnp.dot(d2[s, 1].reshape(2 * half, radial), w[s, radial:], preferred_element_type=F32)
            for c in range(2):
                for q in range(rows_q):
                    part = y[c * half + q * planes : c * half + (q + 1) * planes]
                    walled(out, s, angle(j - 1 + c, q), 0, part, 0)

    def second_step(j):
        @pl.when(j == 0)
        def _():
            take_edges(1)

        explicit(1, j)

        @pl.when(lax.rem(j, 2) == 1)
        def _():
            implicit_second(j)

    inside = max(chunks - 4, 0)

    @pl.loop(0, chunks + 1)
    def _(i):
        @pl.when(i < forwarded)
        def _():
            each_exchange(i, lambda copy: copy.wait_recv())
            pack(lambda side: pkt.at[i, side], t0, i, 0)
            for side in range(2):

                @pl.when(has_to[side])
                def _():
                    own_copy(i, side, False).start()

            @pl.when(i == 0)
            def _():
                send_edges(0)

        if inside:

            @pl.when((i >= 3) & (i < 3 + inside))
            def _():
                second_step(i - 3)

        @pl.when(i >= 1)
        def _():
            @pl.when(i - 1 >= forwarded)
            def _():
                each_exchange(i - 1, lambda copy: copy.wait_recv())

            @pl.when(i == 1)
            def _():
                take_edges(0)

            explicit(0, i - 1)
            implicit_first(i - 1)
            pack(lambda side: pk1.at[i - 1, side, 1], o1, i - 1, 0)
            pack(lambda side: pk1.at[i - 1, side, 0], t1, i - 1, 1)
            for side in range(2):

                @pl.when(has_to[side])
                def _():
                    second_copy(i - 1, side).start()

            @pl.when(i == 1)
            def _():
                send_edges(1)

    @pl.loop(inside, chunks)
    def _(j):
        second_step(j)

    flag_copy().wait_send()
    for step in range(2):
        for side in range(2):
            for copy in ang_copies(step, side):
                copy.wait_send()

    @pl.loop(0, chunks)
    def _(j):
        each_exchange(j, lambda copy: copy.wait_send())
        for side in range(2):

            @pl.when(has_to[side])
            def _():
                other_copy(j, side).wait_send()
                own_copy(j, side, True).wait_send()
                second_copy(j, side).wait_send()


def per_device(
    concentration, courant, axial_diffusion, angular_rate, rate_constants, species_map, wall_flags, radial_inverse
):
    species, angles, planes, radial = concentration.shape
    chunks, rows_q = angles // (2 * H), 2 * H
    packed, half = species * rows_q, rows_q * planes
    hbm, vmem = pl.BlockSpec(memory_space=pltpu.HBM), pl.BlockSpec(memory_space=pltpu.VMEM)
    dma = pltpu.SemaphoreType.DMA
    return pl.pallas_call(
        comm_kernel,
        out_shape=pltpu.VMEM((species, angles, planes, radial), F32),
        in_specs=[hbm] * 8,
        out_specs=vmem,
        scratch_shapes=[
            pltpu.VMEM((1, radial), F32),
            pltpu.VMEM((species, radial), F32),
            pltpu.SMEM(axial_diffusion.shape, F32),
            pltpu.SMEM(rate_constants.shape, F32),
            pltpu.SMEM(species_map.shape, jnp.int32),
            pltpu.VMEM((species, angles), jnp.int32),
            pltpu.VMEM((species, angles + 2, planes, radial), F32),
            pltpu.VMEM((species, angles + 2, planes, radial), F32),
            pltpu.VMEM((species, angles + 2, planes, radial), BF16),
            pltpu.VMEM((species, angles + 2, planes, radial), BF16),
            pltpu.VMEM((species, angles, planes, radial), BF16),
            pltpu.VMEM((species, 3, half, radial), BF16),
            pltpu.VMEM((species, 2, 2, half, radial), BF16),
            pltpu.VMEM((species, 2 * radial, radial), BF16),
            pltpu.VMEM((species, radial, radial), BF16),
            pltpu.VMEM((species, radial, radial), BF16),
            pltpu.VMEM((species, 3, planes, radial), F32),
            pltpu.VMEM((2, 2, packed, radial), F32),
            pltpu.VMEM((2, 2, packed, radial), F32),
            pltpu.VMEM((chunks, 2, packed, radial), BF16),
            pltpu.VMEM((chunks, 2, packed, radial), BF16),
            pltpu.VMEM((chunks, 2, 2, packed, radial), BF16),
            pltpu.VMEM((chunks, 2, 2, packed, radial), BF16),
            pltpu.VMEM((chunks, 2, 2, packed, radial), BF16),
            pltpu.VMEM((2, 2, species, planes, radial), BF16),
            pltpu.VMEM((2, 2, species, planes, radial), BF16),
            pltpu.VMEM((8, LANES), F32),
            pltpu.VMEM((8, LANES), F32),
            pltpu.VMEM((2, species, angles, planes, LANES), F32),
            dma((chunks, 2)),
            dma((chunks, 2)),
            dma((chunks, 2)),
            dma((chunks, 2)),
            dma((chunks, 2)),
            dma((chunks, 2, 2)),
            dma((chunks, 2)),
            dma((chunks, 2)),
            dma((2, 2, 2)),
            dma((2, 2, 2)),
            dma((2,)),
            dma((2,)),
            dma((6,)),
        ],
        compiler_params=pltpu.CompilerParams(
            collective_id=0, has_side_effects=True, vmem_limit_bytes=VMEM_LIMIT
        ),
        name="steps",
    )(
        *(
            pltpu.with_memory_space_constraint(x, pltpu.HBM)
            for x in (
                concentration, courant.reshape(1, radial), angular_rate, axial_diffusion,
                rate_constants, species_map, wall_flags, radial_inverse,
            )
        )
    )


def solution(mesh):
    in_specs = (P(None, "ang", "ax", None), P(), P(), P(), P(), P(), P(None, "ang"), P())
    out_specs = P(None, "ang", "ax", None)
    return jax.shard_map(
        per_device, mesh=mesh, in_specs=in_specs, out_specs=out_specs, check_vma=False
    )
```

```python
import jax
import jax.numpy as jnp
from jax import lax
from jax.experimental import pallas as pl
from jax.experimental.pallas import tpu as pltpu
from jax.sharding import PartitionSpec as P

MESH = pl.DeviceIdType.MESH
F32, BF16 = jnp.float32, jnp.bfloat16
LANES = 128
H = 2
DIRECT = 2
VMEM_LIMIT = 40000000


def comm_kernel(
    conc, courant_in, ang_rate_in, ax_diff_in, rates_in, smap_in, flags_in, rinv,
    out,
    courant, ang_rate, ax_diff, rates, smap, flags,
    o0, o1, t0, t1, ob, d1, d2, w, ma, ml, coef, hxf, pkf, pko, pkt, pk1, hx0, hx1, pa, ha, fl, fl_other, keep,
    load_sem, x_send, x_recv, hxt_send, hxe_send, hx0_recv, hx1_send, hx1_recv, a_send, a_recv, fl_sem, m_sem, p_sem,
):
    species, _, planes, radial = o0.shape
    angles = ob.shape[1]
    chunks = angles // (2 * H)
    rows_q = 2 * H
    per_blk = species * rows_q
    forwarded = chunks - DIRECT
    ang, ax = lax.axis_index("ang"), lax.axis_index("ax")
    n_ang, n_ax = lax.axis_size("ang"), lax.axis_size("ax")
    opp = lax.rem(ang + n_ang // 2, n_ang)
    side_count = n_ang // 2
    place = lax.rem(ang, side_count)
    base = ang - place
    up = base + lax.rem(place + 1, side_count)
    down = base + lax.rem(place + side_count - 1, side_count)
    wraps = (place == side_count - 1, place == 0)
    has_low, has_high = ax > 0, ax < n_ax - 1
    peer = {"ang": opp, "ax": ax}
    ang_peers = ({"ang": up, "ax": ax}, {"ang": down, "ax": ax})
    ax_peers = ({"ang": opp, "ax": ax + 1}, {"ang": opp, "ax": ax - 1})
    ax_own = ({"ang": ang, "ax": ax + 1}, {"ang": ang, "ax": ax - 1})
    has_to, has_from = (has_high, has_low), (has_low, has_high)
    own, other = (o0, o1), (t0, t1)

    def angle(j, q):
        return j * H + q if q < H else angles - (j + 1) * H + q - H

    def remote(source, target, send, recv, device):
        return pltpu.make_async_remote_copy(
            source, target, send, recv, device_id=device, device_id_type=MESH
        )

    def load(j, end):
        start = (j * H, angles - (j + 1) * H)[end]
        return pltpu.make_async_copy(
            conc.at[:, pl.ds(start, H)], o0.at[:, pl.ds(start + 1, H)], load_sem.at[j, end]
        )

    def exchange(j, end, count):
        first = j * H + (0 if count > H else 1)
        start = (first, angles - first - count)[end]
        return remote(
            ob.at[:, pl.ds(start, count)], t0.at[:, pl.ds(start + 1, count)],
            x_send.at[j, end], x_recv.at[j, end], peer,
        )

    def each_exchange(i, act):
        for cond, count in ((i == 0, H + 1), ((i > 0) & (i < chunks - 1), H), (i == chunks - 1, H - 1)):

            @pl.when(cond)
            def _():
                act(exchange(i, 0, count))
                act(exchange(i, 1, count))

    def other_copy(j, side):
        return remote(
            pko.at[j, side], hx0.at[j, side, 1], hxt_send.at[j, side], hx0_recv.at[j, side, 1], ax_peers[side]
        )

    def own_copy(j, side, direct):
        return remote(
            (pko if direct else pkt).at[j, side], hx0.at[j, side, 0],
            hxe_send.at[j, side], hx0_recv.at[j, side, 0], (ax_own if direct else ax_peers)[side],
        )

    def second_copy(j, side):
        return remote(
            pk1.at[j, side], hx1.at[j, side], hx1_send.at[j, side], hx1_recv.at[j, side], ax_peers[side]
        )

    def ang_copies(step, side, swapped=0):
        t = other[step]
        source, target = ((angles, 0), (1, angles + 1))[side]
        targets = (ha.at[step, side], t.at[:, target])
        return tuple(
            remote(
                start, targets[n ^ swapped], a_send.at[step, side, n], a_recv.at[step, side, n ^ swapped], ang_peers[side]
            )
            for n, start in enumerate((pa.at[step, side], t.at[:, source]))
        )

    def flag_copy():
        return remote(fl, fl_other, fl_sem.at[0], fl_sem.at[1], peer)

    barrier = pltpu.get_barrier_semaphore()
    for device in (peer, *ang_peers):
        pl.semaphore_signal(barrier, inc=1, device_id=device, device_id_type=MESH)
    for side in range(2):

        @pl.when(has_to[side])
        def _():
            pl.semaphore_signal(barrier, inc=1, device_id=ax_peers[side], device_id_type=MESH)
            pl.semaphore_signal(barrier, inc=1, device_id=ax_own[side], device_id_type=MESH)

    for j in range(chunks):
        load(j, 0).start()
        load(j, 1).start()
    small = [
        pltpu.make_async_copy(source, target, p_sem.at[n])
        for n, (source, target) in enumerate((
            (courant_in, courant), (ang_rate_in, ang_rate), (ax_diff_in, ax_diff),
            (rates_in, rates), (smap_in, smap), (flags_in, flags),
        ))
    ]
    for copy in small:
        copy.start()
    load_a = pltpu.make_async_copy(rinv.at[:, :radial, :radial], ma, m_sem.at[0])
    load_l = pltpu.make_async_copy(rinv.at[:, radial:, :radial], ml, m_sem.at[1])
    load_a.start()
    load_l.start()

    def cast(j):
        for end in range(2):
            load(j, end).wait()
            start = (j * H, angles - (j + 1) * H)[end]
            for i in range(H):
                for s in range(species):
                    ob[s, start + i] = o0[s, start + i + 1].astype(BF16)

    cast(0)
    cast(1)
    for copy in small:
        copy.wait()
    fl[...] = jnp.zeros_like(fl)
    fl[:species, :angles] = flags[...].astype(F32)
    pl.semaphore_wait(barrier, 3 + jnp.where(has_low, 2, 0) + jnp.where(has_high, 2, 0))
    def pack(target, ref, j, per):
        for q in range(rows_q):
            a = angle(j, q) + 1
            for s in range(species):
                value = ref[s, a].astype(F32)
                row = slice(s * rows_q + q, s * rows_q + q + 1)
                pkf[per, 0, row, :] = value[planes - 1 : planes]
                pkf[per, 1, row, :] = value[0:1]
        for side in range(2):
            target(side)[...] = pkf[per, side].astype(BF16)

    def send(j):
        count = H + 1 if j == 0 else H if j < chunks - 1 else H - 1
        exchange(j, 0, count).start()
        exchange(j, 1, count).start()

    def send_planes(j, direct):
        pack(lambda side: pko.at[j, side], o0, j, 0)
        for side in range(2):

            @pl.when(has_to[side])
            def _():
                other_copy(j, side).start()
                if direct:
                    own_copy(j, side, True).start()

    flag_copy().start()
    send(0)
    for j in range(2, chunks):
        cast(j)
    for j in range(forwarded, chunks):
        send_planes(j, True)
    for j in range(1, chunks):
        send(j)

    @pl.loop(0, forwarded)
    def _(j):
        send_planes(j, False)

    for s in range(species):
        diffusion = ax_diff[s]
        coef[s, 0] = jnp.broadcast_to(
            1.0 - courant[...] - 2.0 * diffusion - 2.0 * ang_rate[s : s + 1], (planes, radial)
        )
        coef[s, 1] = jnp.broadcast_to(courant[...] + diffusion, (planes, radial))
        coef[s, 2] = jnp.broadcast_to(ang_rate[s : s + 1], (planes, radial))
    for side in range(2):

        @pl.when(jnp.logical_not(has_from[side]))
        def _():
            @pl.loop(0, chunks)
            def _(j):
                hx0[j, side] = jnp.zeros(hx0.shape[2:], BF16)
                hx1[j, side] = jnp.zeros(hx1.shape[2:], BF16)

    gains = []
    for p in range(species):
        gain = jnp.float32(0.0)
        for k in range(rates.shape[0]):
            gain = gain + jnp.where(smap[k, 2] == p, rates[k], jnp.float32(0.0))
        gains.append(gain)

    load_a.wait()
    load_l.wait()
    flip = (
        lax.broadcasted_iota(jnp.int32, (radial, radial), 0)
        + lax.broadcasted_iota(jnp.int32, (radial, radial), 1)
        == radial - 1
    )
    flip = jnp.where(flip, 1.0, 0.0).astype(BF16)
    for s in range(species):
        w[s, :radial] = ma[s].T
        w[s, radial:] = jnp.dot(ml[s].T, flip, preferred_element_type=F32).astype(BF16)

    flag_copy().wait_recv()
    diagonal = lax.broadcasted_iota(jnp.int32, (angles, LANES), 0) == lax.broadcasted_iota(
        jnp.int32, (angles, LANES), 1
    )
    for blk, ref in enumerate((fl, fl_other)):
        for s in range(species):
            row = jnp.broadcast_to(ref[s : s + 1], (angles, LANES))
            column = jnp.sum(jnp.where(diagonal, row, 0.0), axis=1, keepdims=True)
            rows = jnp.broadcast_to(1.0 - column, (angles, LANES))
            for a in range(angles):
                keep[blk, s, a] = jnp.broadcast_to(rows[a : a + 1], (planes, LANES))

    lane0 = lax.broadcasted_iota(jnp.int32, (planes, LANES), 1) == 0
    plane = lax.broadcasted_iota(jnp.int32, (planes, LANES), 0)
    first, last = plane == 0, plane == planes - 1
    half = rows_q * planes

    def send_edges(step):
        for side in range(2):
            source = (angles, 1)[side]
            for s in range(species):
                pa[step, side, s] = own[step][s, source].astype(BF16)
            for swapped in range(2):

                @pl.when(wraps[side] if swapped else jnp.logical_not(wraps[side]))
                def _():
                    for copy in ang_copies(step, side, swapped):
                        copy.start()

    def take_edges(step):
        for side in range(2):
            for copy in ang_copies(step, side):
                copy.wait_recv()
            target = (0, angles + 1)[side]
            for s in range(species):
                own[step][s, target] = ha[step, side, s].astype(F32)

    def explicit(step, j):
        for side in range(2):

            @pl.when(has_from[side])
            def _():
                if step:
                    second_copy(j, side).wait_recv()
                else:
                    own_copy(j, side, True).wait_recv()
                    other_copy(j, side).wait_recv()

            for blk in range(2):
                hxf[side, blk] = (hx0, hx1)[step][j, side, blk].astype(F32)
        for q in range(rows_q):
            a = angle(j, q) + 1
            for blk, ref in ((0, own[step]), (1, other[step])):
                for lane in range(0, radial, LANES):
                    sl = pl.ds(lane, LANES)
                    f = [ref[s, a, :, sl].astype(F32) for s in range(species)]
                    terms = [
                        gains[s] * (f[(s + 1) % species] * f[(s + 2) % species])
                        for s in range(species)
                    ]
                    total = terms[0] + terms[1] + terms[2]
                    for s in range(species):
                        row = slice(s * rows_q + q, s * rows_q + q + 1)
                        before = jnp.where(first, hxf[0, blk, row, sl], pltpu.roll(f[s], 1, 0))
                        after = jnp.where(last, hxf[1, blk, row, sl], pltpu.roll(f[s], planes - 1, 0))
                        angular = ref[s, a - 1, :, sl].astype(F32) + ref[s, a + 1, :, sl].astype(F32)
                        value = (
                            coef[s, 0, :, sl] * f[s]
                            + coef[s, 1, :, sl] * before
                            + ax_diff[s] * after
                            + coef[s, 2, :, sl] * angular
                            + (2.0 * terms[s] - total)
                        ).astype(BF16)
                        rows = pl.ds(q * planes, planes)
                        if step:
                            d2[s, blk, lax.rem(j, 2), rows, sl] = value
                        else:
                            d1[s, blk, rows, sl] = value
                            if blk == 0:
                                d1[s, 2, rows, sl] = value

    def walled(ref, s, a, blk, part, offset):
        head = part[:, :LANES]
        wall = pltpu.roll(head, LANES - 1, 1) * keep[blk, s, a]
        ref[s, a + offset, :, :LANES] = jnp.where(lane0, wall, head).astype(ref.dtype)
        ref[s, a + offset, :, LANES:] = part[:, LANES:].astype(ref.dtype)

    def implicit_first(j):
        for s in range(species):
            mine = d1[s, :2].reshape(2 * half, radial)
            theirs = d1[s, 1:].reshape(2 * half, radial)
            y = jnp.dot(mine, w[s, :radial], preferred_element_type=F32)
            y = y + jnp.dot(theirs, w[s, radial:], preferred_element_type=F32)
            for blk, ref in ((0, o1), (1, t1)):
                for q in range(rows_q):
                    part = y[blk * half + q * planes : blk * half + (q + 1) * planes]
                    walled(ref, s, angle(j, q), blk, part, 1)

    def implicit_second(j):
        for s in range(species):
            y = jnp.dot(d2[s, 0].reshape(2 * half, radial), w[s, :radial], preferred_element_type=F32)
            y = y + jnp.dot(d2[s, 1].reshape(2 * half, radial), w[s, radial:], preferred_element_type=F32)
            for c in range(2):
                for q in range(rows_q):
                    part = y[c * half + q * planes : c * half + (q + 1) * planes]
                    walled(out, s, angle(j - 1 + c, q), 0, part, 0)

    def second_step(j):
        @pl.when(j == 0)
        def _():
            take_edges(1)

        explicit(1, j)

        @pl.when(lax.rem(j, 2) == 1)
        def _():
            implicit_second(j)

    inside = max(chunks - 4, 0)

    @pl.loop(0, chunks + 1)
    def _(i):
        @pl.when(i < forwarded)
        def _():
            each_exchange(i, lambda copy: copy.wait_recv())
            pack(lambda side: pkt.at[i, side], t0, i, 0)
            for side in range(2):

                @pl.when(has_to[side])
                def _():
                    own_copy(i, side, False).start()

            @pl.when(i == 0)
            def _():
                send_edges(0)

        if inside:

            @pl.when((i >= 3) & (i < 3 + inside))
            def _():
                second_step(i - 3)

        @pl.when(i >= 1)
        def _():
            @pl.when(i - 1 >= forwarded)
            def _():
                each_exchange(i - 1, lambda copy: copy.wait_recv())

            @pl.when(i == 1)
            def _():
                take_edges(0)

            explicit(0, i - 1)
            implicit_first(i - 1)
            pack(lambda side: pk1.at[i - 1, side, 1], o1, i - 1, 0)
            pack(lambda side: pk1.at[i - 1, side, 0], t1, i - 1, 1)
            for side in range(2):

                @pl.when(has_to[side])
                def _():
                    second_copy(i - 1, side).start()

            @pl.when(i == 1)
            def _():
                send_edges(1)

    @pl.loop(inside, chunks)
    def _(j):
        second_step(j)

    flag_copy().wait_send()
    for step in range(2):
        for side in range(2):
            for copy in ang_copies(step, side):
                copy.wait_send()

    @pl.loop(0, chunks)
    def _(j):
        each_exchange(j, lambda copy: copy.wait_send())
        for side in range(2):

            @pl.when(has_to[side])
            def _():
                other_copy(j, side).wait_send()
                own_copy(j, side, True).wait_send()
                second_copy(j, side).wait_send()


def per_device(
    concentration, courant, axial_diffusion, angular_rate, rate_constants, species_map, wall_flags, radial_inverse
):
    species, angles, planes, radial = concentration.shape
    chunks, rows_q = angles // (2 * H), 2 * H
    packed, half = species * rows_q, rows_q * planes
    hbm, vmem = pl.BlockSpec(memory_space=pltpu.HBM), pl.BlockSpec(memory_space=pltpu.VMEM)
    dma = pltpu.SemaphoreType.DMA
    return pl.pallas_call(
        comm_kernel,
        out_shape=pltpu.VMEM((species, angles, planes, radial), F32),
        in_specs=[hbm] * 8,
        out_specs=vmem,
        scratch_shapes=[
            pltpu.VMEM((1, radial), F32),
            pltpu.VMEM((species, radial), F32),
            pltpu.SMEM(axial_diffusion.shape, F32),
            pltpu.SMEM(rate_constants.shape, F32),
            pltpu.SMEM(species_map.shape, jnp.int32),
            pltpu.VMEM((species, angles), jnp.int32),
            pltpu.VMEM((species, angles + 2, planes, radial), F32),
            pltpu.VMEM((species, angles + 2, planes, radial), F32),
            pltpu.VMEM((species, angles + 2, planes, radial), BF16),
            pltpu.VMEM((species, angles + 2, planes, radial), BF16),
            pltpu.VMEM((species, angles, planes, radial), BF16),
            pltpu.VMEM((species, 3, half, radial), BF16),
            pltpu.VMEM((species, 2, 2, half, radial), BF16),
            pltpu.VMEM((species, 2 * radial, radial), BF16),
            pltpu.VMEM((species, radial, radial), BF16),
            pltpu.VMEM((species, radial, radial), BF16),
            pltpu.VMEM((species, 3, planes, radial), F32),
            pltpu.VMEM((2, 2, packed, radial), F32),
            pltpu.VMEM((2, 2, packed, radial), F32),
            pltpu.VMEM((chunks, 2, packed, radial), BF16),
            pltpu.VMEM((chunks, 2, packed, radial), BF16),
            pltpu.VMEM((chunks, 2, 2, packed, radial), BF16),
            pltpu.VMEM((chunks, 2, 2, packed, radial), BF16),
            pltpu.VMEM((chunks, 2, 2, packed, radial), BF16),
            pltpu.VMEM((2, 2, species, planes, radial), BF16),
            pltpu.VMEM((2, 2, species, planes, radial), BF16),
            pltpu.VMEM((8, LANES), F32),
            pltpu.VMEM((8, LANES), F32),
            pltpu.VMEM((2, species, angles, planes, LANES), F32),
            dma((chunks, 2)),
            dma((chunks, 2)),
            dma((chunks, 2)),
            dma((chunks, 2)),
            dma((chunks, 2)),
            dma((chunks, 2, 2)),
            dma((chunks, 2)),
            dma((chunks, 2)),
            dma((2, 2, 2)),
            dma((2, 2, 2)),
            dma((2,)),
            dma((2,)),
            dma((6,)),
        ],
        compiler_params=pltpu.CompilerParams(
            collective_id=0, has_side_effects=True, vmem_limit_bytes=VMEM_LIMIT
        ),
        name="steps",
    )(
        *(
            pltpu.with_memory_space_constraint(x, pltpu.HBM)
            for x in (
                concentration, courant.reshape(1, radial), angular_rate, axial_diffusion,
                rate_constants, species_map, wall_flags, radial_inverse,
            )
        )
    )


def solution(mesh):
    in_specs = (P(None, "ang", "ax", None), P(), P(), P(), P(), P(), P(None, "ang"), P())
    out_specs = P(None, "ang", "ax", None)
    return jax.shard_map(
        per_device, mesh=mesh, in_specs=in_specs, out_specs=out_specs, check_vma=False
    )
```
